512 devices in a mesh: row: 16 (over x_hi, z), col: 32 (over x_lo, y, core).
Axes of the slice: x: 4 (x_hi: 2, x_lo: 2; x = x_hi * 2 + x_lo), y: 8, z: 8, core: 2. Of those that a mesh axis runs over, the one named last changes fastest.
Arguments:
- slots: bfloat16 [3072, 128, 128], P(('row', 'col')), may hold values from -6 to 6
- block_list: int32 [3072], P(('row', 'col')), may hold values from -1 to 15, as said below
- metric: bfloat16 [8192, 4096], P('row', 'col'), may hold values from -0.125 to 0.125
Outputs:
- contracted: float32 [16384, 4096], P('row', 'col')
The draws below stay inside these ranges and needn't reach their ends.
Inputs may be any that keep to these rules, and one draw needn't show every extreme that they name: `block_list`: the live entries of one device's 6 slots come first and name distinct blocks; -1 marks an unused slot; every device has at least 3 live slots and some device has all 6 live.
All inputs are finite; a program needn't handle non-finite values.
Results may differ from the reference program's by a relative error of at most 0.0003.
Values may be sent and summed in bfloat16 or wider, within the bound.
No kernel may reach another device: no remote copies, remote signals or barrier semaphores. Data moves between devices by JAX's collectives and lax.ppermute only.
A program may use at most 128 MiB of HBM per device.

```python
import jax
import jax.numpy as jnp
from jax import lax

BLK = 128
PAIR_DEV = 1024
KMAX = 6
NP = 8192
NPAIR = 16384
NQ = 4096
N_ROW = 16
N_COL = 32


def draw_block_list(key, part):
    device_count = N_ROW * N_COL
    tile_blocks = PAIR_DEV // BLK * (NP // N_COL // BLK)
    first_key = jax.random.fold_in(key, 11)
    second_key = jax.random.fold_in(key, 23)
    third_key = jax.random.fold_in(key, 37)
    scores = jax.random.randint(first_key, (device_count, tile_blocks), 0, 1 << 20) * tile_blocks
    scores = scores + jnp.arange(tile_blocks, dtype=jnp.int32)[None, :]
    picked = jnp.argsort(scores, axis=1)[:, :KMAX].astype(jnp.int32)
    counts = jax.random.randint(second_key, (device_count,), (KMAX + 1) // 2, KMAX + 1)
    forced = jax.random.randint(third_key, (), 0, device_count)
    counts = jnp.where(jnp.arange(device_count) == forced, KMAX, counts)
    is_live = jnp.arange(KMAX)[None, :] < counts[:, None]
    return jnp.where(is_live, picked, -1).astype(jnp.int32).reshape(-1)


def levels(own_key, shape, shards, least, top_value):
    factor_of, own = 1.0, jax.random.fold_in(own_key, 6)
    for axis_at, shards_of in shards:
        steps = jnp.exp(jax.random.uniform(jax.random.fold_in(own, axis_at), (shards_of,), jnp.float32, least / len(shards), top_value / len(shards)))
        factor_of = factor_of * jnp.repeat(steps, shape[axis_at] // shards_of).reshape([-1 if axis == axis_at else 1 for axis in range(len(shape))])
    return factor_of


def normal_values(stream_key, dims, width, limit, split=(), held_as=jnp.bfloat16):
    values = width * jax.random.normal(stream_key, dims, jnp.float32)
    if split:
        values = values * levels(stream_key, dims, split, -0.22, 0.18)
    return jnp.clip(values, -limit, limit).astype(held_as)


def setup_inputs(seed: int = 0) -> dict:
    arg_keys = jax.random.split(jax.random.key(seed), 4)
    slots = normal_values(arg_keys[0], (N_ROW * N_COL * KMAX, BLK, BLK), 1.0, 6.0, ((0, 512),))
    block_list = draw_block_list(jax.random.fold_in(arg_keys[3], 71), 0)
    metric = normal_values(arg_keys[2], (NP, NQ), (NP // 4) ** -0.5, 0.125, ((0, 16), (1, 32)))
    return {"slots": slots, "block_list": block_list, "metric": metric}


def reference(slots, block_list, metric):
    pair_blocks = PAIR_DEV // BLK
    col_blocks = NP // N_COL // BLK
    slot_grid = slots.reshape(N_ROW, N_COL * KMAX, BLK, BLK)
    list_grid = block_list.reshape(N_ROW, N_COL * KMAX)
    metric_blocks = metric.reshape(NP // BLK, BLK, NQ)
    shard_of = (jnp.arange(N_COL * KMAX) // KMAX).astype(jnp.int32)

    def one_band(inputs):
        band_slots, band_list = inputs
        clipped = jnp.maximum(band_list, 0)
        is_live = band_list >= 0
        global_block = (shard_of * col_blocks + clipped % col_blocks).astype(jnp.int32)
        pair_block = (clipped // col_blocks).astype(jnp.int32)

        def add_slot(total, entry):
            block, glob, pairb, alive = entry
            rows = metric_blocks[glob]
            prod = jnp.dot(block, rows, preferred_element_type=jnp.float32)
            prod = jnp.where(alive, prod, jnp.zeros_like(prod))
            begin = (pairb * BLK).astype(jnp.int32)
            current = lax.dynamic_slice_in_dim(total, begin, BLK, 0)
            total = lax.dynamic_update_slice_in_dim(total, current + prod, begin, 0)
            return total, None

        start_total = jnp.zeros((PAIR_DEV, NQ), jnp.float32)
        total, _ = lax.scan(add_slot, start_total, (band_slots, global_block, pair_block, is_live))
        return total

    bands = lax.map(one_band, (slot_grid, list_grid))
    return bands.reshape(NPAIR, NQ)
```

```python
import jax
import jax.numpy as jnp
from jax import lax
from jax.experimental import pallas as pl
from jax.experimental.pallas import tpu as pltpu
from jax.sharding import PartitionSpec as P

BLK = 128
PAIR_DEV = 1024
PAIR_BLOCKS = PAIR_DEV // BLK
KMAX = 6
NY = 8
LIST_ROWS = 16
SLOT_ROWS = KMAX * BLK
P_LANE = 8


def col_of(x, y, core):
    return ((x % 2) * NY + y % NY) * 2 + core % 2


def col_perm(target):
    return [
        (col_of(x, y, c), col_of(*target(x, y, c)))
        for x in range(2)
        for y in range(NY)
        for c in range(2)
    ]


CORE = col_perm(lambda x, y, c: (x, y, c + 1))
X_PARTNER = col_perm(lambda x, y, c: (x + 1, y, c))
RING = col_perm(lambda x, y, c: (x, y + 1 if c == 0 else y - 1, c))


def sent(value, perm, axis="col"):
    return lax.ppermute(value, axis, perm)


def payload(slots, block_list, col_blocks):
    me = lax.axis_index("col")
    clipped = jnp.maximum(block_list, 0)
    band_block = me * col_blocks + clipped % col_blocks
    pair_block = jnp.where(block_list >= 0, clipped // col_blocks, PAIR_BLOCKS)
    row = jnp.concatenate(
        [
            jnp.pad(band_block, (0, P_LANE - KMAX)),
            jnp.pad(pair_block, (0, BLK - P_LANE - KMAX)),
        ]
    )
    rows = jnp.broadcast_to(row.astype(jnp.bfloat16), (LIST_ROWS, BLK))
    return jnp.concatenate([slots.reshape(SLOT_ROWS, BLK), rows])[None]


def add_products(metric_ref, piece_refs, total, metric_v, pieces_v, rows_v, list_v, list_s, sems, prepare):
    starts = [sum(ref.shape[0] for ref in piece_refs[:n]) for n in range(len(piece_refs))]
    places = [pl.ds(start, ref.shape[0]) for start, ref in zip(starts, piece_refs)]
    list_rows = [
        pltpu.make_async_copy(ref.at[:, SLOT_ROWS:, :], rows_v.at[place], sems.at[0, n])
        for n, (ref, place) in enumerate(zip(piece_refs, places))
    ]
    metric_copy = pltpu.make_async_copy(metric_ref, metric_v, sems.at[1, len(piece_refs)])
    piece_copies = [
        pltpu.make_async_copy(ref.at[:, :SLOT_ROWS, :], pieces_v.at[place], sems.at[1, n])
        for n, (ref, place) in enumerate(zip(piece_refs, places))
    ]
    for copy in (*list_rows, metric_copy, *piece_copies):
        copy.start()
    prepare()
    for copy in list_rows:
        copy.wait()
    for i in range(rows_v.shape[0]):
        rows = rows_v[i].astype(jnp.float32)
        list_v[i : i + 1, :] = rows[:1].astype(jnp.int32)
    list_copy = pltpu.make_async_copy(list_v, list_s, sems.at[0, len(piece_refs)])
    list_copy.start()
    list_copy.wait()
    metric_copy.wait()

    def one_piece(i, carry):
        for j in range(KMAX):
            band_block = list_s[i, j]
            pair_block = list_s[i, P_LANE + j]
            prod = jnp.dot(
                pieces_v[i, j * BLK : (j + 1) * BLK, :],
                metric_v[band_block],
                preferred_element_type=jnp.float32,
            )
            total[pair_block] += prod
        return carry

    for copy, start, ref in zip(piece_copies, starts, piece_refs):
        copy.wait()
        lax.fori_loop(start, start + ref.shape[0], one_piece, 0)


def early_products(metric_ref, *refs):
    *piece_refs, total, metric_v, pieces_v, rows_v, list_v, list_s, sems = refs

    def clear():
        total[...] = jnp.zeros_like(total)

    add_products(metric_ref, piece_refs, total, metric_v, pieces_v, rows_v, list_v, list_s, sems, clear)


def late_products(early_ref, metric_ref, *refs):
    *piece_refs, out_ref, total, metric_v, pieces_v, rows_v, list_v, list_s, sems = refs

    def take():
        total[...] = early_ref[...]

    add_products(metric_ref, piece_refs, total, metric_v, pieces_v, rows_v, list_v, list_s, sems, take)
    for p in range(PAIR_BLOCKS):
        out_ref[p * BLK : (p + 1) * BLK, :] = total[p]


def kernel_call(body, out_shape, taken, metric, pieces, scratch):
    vmem = pl.BlockSpec(memory_space=pltpu.VMEM)
    count = sum(piece.shape[0] for piece in pieces)
    return pl.pallas_call(
        body,
        out_shape=out_shape,
        in_specs=[vmem] * len(taken) + [pl.BlockSpec(memory_space=pltpu.HBM)] * (1 + len(pieces)),
        out_specs=vmem,
        scratch_shapes=[
            *scratch,
            pltpu.VMEM(metric.shape, metric.dtype),
            pltpu.VMEM((count, SLOT_ROWS, BLK), metric.dtype),
            pltpu.VMEM((count, LIST_ROWS, BLK), metric.dtype),
            pltpu.VMEM((count, BLK), jnp.int32),
            pltpu.SMEM((count, BLK), jnp.int32),
            pltpu.SemaphoreType.DMA((2, len(pieces) + 1)),
        ],
        compiler_params=pltpu.CompilerParams(vmem_limit_bytes=60 << 20),
    )(*taken, metric, *pieces)


def on_device(slots, block_list, metric):
    out_cols = metric.shape[1]
    rows = lax.axis_size("row")
    band_blocks = rows * metric.shape[0] // BLK
    col_blocks = band_blocks // lax.axis_size("col")
    copies = jnp.broadcast_to(metric, (rows, *metric.shape))
    band = lax.all_to_all(copies, "row", split_axis=0, concat_axis=0, tiled=True)
    band = band.reshape(band_blocks, BLK, out_cols)

    own = payload(slots, block_list, col_blocks)
    own_x = sent(own, X_PARTNER)
    near = jnp.concatenate([own, sent(own, CORE)])
    near_x = jnp.concatenate([own_x, sent(own_x, CORE)])
    a1 = sent(near, RING)
    b1 = sent(near_x, RING)
    a2 = sent(a1, RING)
    b2 = sent(b1, RING)
    a3 = sent(a2, RING)
    a4 = sent(a3[:1], RING)
    early = [a1, b1, a2, b2, a3]
    late = [sent(a3, X_PARTNER), a4, sent(a4, X_PARTNER)]
    early_other = sent(jnp.concatenate(early), CORE)
    late_other = sent(jnp.concatenate(late), CORE)
    early = [near, near_x, *early, early_other]
    late = [*late, late_other]
    total_shape = (PAIR_BLOCKS + 1, BLK, out_cols)
    total = kernel_call(
        early_products, jax.ShapeDtypeStruct(total_shape, jnp.float32), [], band, early, []
    )
    return kernel_call(
        late_products,
        jax.ShapeDtypeStruct((PAIR_DEV, out_cols), jnp.float32),
        [total],
        band,
        late,
        [pltpu.VMEM(total_shape, jnp.float32)],
    )


def solution(mesh):
    return jax.shard_map(
        on_device,
        mesh=mesh,
        in_specs=(P(("row", "col"), None, None), P(("row", "col")), P("row", "col")),
        out_specs=P("row", "col"),
        check_vma=False,
    )
```

```python
import functools

import jax
import jax.numpy as jnp
from jax import lax
from jax.experimental import pallas as pl
from jax.experimental.pallas import tpu as pltpu
from jax.sharding import PartitionSpec as P

BLK = 128
PAIR_DEV = 1024
PAIR_BLOCKS = PAIR_DEV // BLK
KMAX = 6
NY = 8
NZ = 8
LIST_ROWS = 16
SLOT_ROWS = KMAX * BLK
P_LANE = 8


def col_of(x, y, core):
    return ((x % 2) * NY + y % NY) * 2 + core % 2


def col_perm(target):
    return [
        (col_of(x, y, c), col_of(*target(x, y, c)))
        for x in range(2)
        for y in range(NY)
        for c in range(2)
    ]


CORE = col_perm(lambda x, y, c: (x, y, c + 1))
X_PARTNER = col_perm(lambda x, y, c: (x + 1, y, c))
RING = col_perm(lambda x, y, c: (x, y + 1 if c == 0 else y - 1, c))


def row_of(x, z):
    return (x % 2) * NZ + z % NZ


def row_perm(step):
    return [(row_of(x, z), row_of(x, z + step)) for x in range(2) for z in range(NZ)]


BAND_GROUPS = [[row_of(x, z) for x in range(2) for z in range(first, NZ, 2)] for first in range(2)]


def sent(value, perm, axis="col"):
    return lax.ppermute(value, axis, perm)


def payload(slots, block_list, col_blocks, shard_blocks):
    me = lax.axis_index("col")
    clipped = jnp.maximum(block_list, 0)
    shard = me * col_blocks // shard_blocks
    x, z = shard // NZ, shard % NZ
    place = (z % 2) * NZ + x * (NZ // 2) + z // 2
    band_block = place * shard_blocks + me * col_blocks % shard_blocks + clipped % col_blocks
    pair_block = jnp.where(block_list >= 0, clipped // col_blocks, PAIR_BLOCKS)
    row = jnp.concatenate(
        [
            jnp.pad(band_block, (0, P_LANE - KMAX)),
            jnp.pad(pair_block, (0, BLK - P_LANE - KMAX)),
        ]
    )
    rows = jnp.broadcast_to(row.astype(jnp.bfloat16), (LIST_ROWS, BLK))
    return jnp.concatenate([slots.reshape(SLOT_ROWS, BLK), rows])[None]


def add_products(pieces_refs, band_refs, total, band_v, pieces_v, rows_v, list_v, list_s, sems, prepare):
    def copies(refs, target, row, take):
        start, made = 0, []
        for n, ref in enumerate(refs):
            count = ref.shape[0]
            made.append(pltpu.make_async_copy(take(ref), target.at[pl.ds(start, count)], sems.at[row, n]))
            start += count
        return made

    list_rows = copies(pieces_refs, rows_v, 0, lambda ref: ref.at[:, SLOT_ROWS:, :])
    band_copies = copies(band_refs, band_v, 1, lambda ref: ref)
    piece_copies = copies(pieces_refs, pieces_v, 2, lambda ref: ref.at[:, :SLOT_ROWS, :])
    for copy in (*list_rows, *band_copies, *piece_copies):
        copy.start()
    prepare()
    for copy in list_rows:
        copy.wait()
    odd = lax.axis_index("row") % 2
    half = band_v.shape[0] // 2
    lanes = lax.broadcasted_iota(jnp.int32, (1, BLK), 1)
    flip = jnp.where(lanes < P_LANE, odd * half, 0)
    for i in range(rows_v.shape[0]):
        rows = rows_v[i].astype(jnp.float32)
        list_v[i : i + 1, :] = jnp.bitwise_xor(rows[:1].astype(jnp.int32), flip)
    list_copy = pltpu.make_async_copy(list_v, list_s, sems.at[3, 0])
    list_copy.start()
    list_copy.wait()
    for copy in band_copies:
        copy.wait()

    def one_piece(i, carry):
        for j in range(KMAX):
            band_block = list_s[i, j]
            pair_block = list_s[i, P_LANE + j]
            prod = jnp.dot(
                pieces_v[i, j * BLK : (j + 1) * BLK, :],
                band_v[band_block],
                preferred_element_type=jnp.float32,
            )
            total[pair_block] += prod
        return carry

    start = 0
    for copy, ref in zip(piece_copies, pieces_refs):
        copy.wait()
        lax.fori_loop(start, start + ref.shape[0], one_piece, 0)
        start += ref.shape[0]


def early_products(count, *refs):
    total, *scratch = refs[-7:]

    def clear():
        total[...] = jnp.zeros_like(total)

    add_products(refs[:count], refs[count:-7], total, *scratch, clear)


def late_products(count, early_ref, *refs):
    out_ref, total, *scratch = refs[-8:]

    def take():
        total[...] = early_ref[...]

    add_products(refs[:count], refs[count:-8], total, *scratch, take)
    for p in range(PAIR_BLOCKS):
        out_ref[p * BLK : (p + 1) * BLK, :] = total[p]


def kernel_call(body, out_shape, taken, pieces, band, scratch):
    vmem = pl.BlockSpec(memory_space=pltpu.VMEM)
    count = sum(piece.shape[0] for piece in pieces)
    blocks = sum(part.shape[0] for part in band)
    dtype = pieces[0].dtype
    return pl.pallas_call(
        functools.partial(body, len(pieces)),
        out_shape=out_shape,
        in_specs=[vmem] * len(taken)
        + [pl.BlockSpec(memory_space=pltpu.HBM)] * (len(pieces) + len(band)),
        out_specs=vmem,
        scratch_shapes=[
            *scratch,
            pltpu.VMEM((blocks, BLK, BLK), dtype),
            pltpu.VMEM((count, SLOT_ROWS, BLK), dtype),
            pltpu.VMEM((count, LIST_ROWS, BLK), dtype),
            pltpu.VMEM((count, BLK), jnp.int32),
            pltpu.SMEM((count, BLK), jnp.int32),
            pltpu.SemaphoreType.DMA((4, max(len(pieces), len(band)))),
        ],
        compiler_params=pltpu.CompilerParams(vmem_limit_bytes=60 << 20),
    )(*taken, *pieces, *band)


def gathered_band(metric):
    copies = jnp.broadcast_to(metric, (NZ, *metric.shape))
    same = lax.all_to_all(
        copies, "row", split_axis=0, concat_axis=0, tiled=True, axis_index_groups=BAND_GROUPS
    )
    upper, lower = same[: NZ // 2], same[NZ // 2 :]
    parts = [same, sent(upper, row_perm(1), "row"), sent(lower, row_perm(-1), "row")]
    return [part.reshape(-1, BLK, metric.shape[1]) for part in parts]


def on_device(slots, block_list, metric):
    out_cols = metric.shape[1]
    rows = lax.axis_size("row")
    band_blocks = rows * metric.shape[0] // BLK
    col_blocks = band_blocks // lax.axis_size("col")
    band = gathered_band(metric)
    own = payload(slots, block_list, col_blocks, metric.shape[0] // BLK)
    own_x = sent(own, X_PARTNER)
    near = jnp.concatenate([own, sent(own, CORE)])
    near_x = jnp.concatenate([own_x, sent(own_x, CORE)])
    a1 = sent(near, RING)
    b1 = sent(near_x, RING)
    a2 = sent(a1, RING)
    b2 = sent(b1, RING)
    a3 = sent(a2, RING)
    b3 = sent(b2, RING)
    a4 = sent(a3[:1], RING)
    b4 = sent(b3[:1], RING)
    early = [a1, b1, a2, b2, a3]
    late = [b3, a4, b4]
    early_other = sent(jnp.concatenate(early), CORE)
    late_other = sent(jnp.concatenate(late), CORE)
    early = [near, near_x, *early, early_other]
    late = [*late, late_other]
    total_shape = (PAIR_BLOCKS + 1, BLK, out_cols)
    total = kernel_call(
        early_products, jax.ShapeDtypeStruct(total_shape, jnp.float32), [], early, band, []
    )
    return kernel_call(
        late_products,
        jax.ShapeDtypeStruct((PAIR_DEV, out_cols), jnp.float32),
        [total],
        late,
        band,
        [pltpu.VMEM(total_shape, jnp.float32)],
    )


def solution(mesh):
    return jax.shard_map(
        on_device,
        mesh=mesh,
        in_specs=(P(("row", "col"), None, None), P(("row", "col")), P("row", "col")),
        out_specs=P("row", "col"),
        check_vma=False,
    )
```

```python
import jax
import jax.numpy as jnp
from jax import lax
from jax.experimental import pallas as pl
from jax.experimental.pallas import tpu as pltpu
from jax.sharding import PartitionSpec as P

BLK = 128
PAIR_DEV = 1024
PAIR_BLOCKS = PAIR_DEV // BLK
KMAX = 6
NY = 8
LIST_ROWS = 16
SLOT_ROWS = KMAX * BLK
P_LANE = 8


def col_of(x, y, core):
    return ((x % 2) * NY + y % NY) * 2 + core % 2


def col_perm(target):
    return [
        (col_of(x, y, c), col_of(*target(x, y, c)))
        for x in range(2)
        for y in range(NY)
        for c in range(2)
    ]


CORE = col_perm(lambda x, y, c: (x, y, c + 1))
X_PARTNER = col_perm(lambda x, y, c: (x + 1, y, c))
RING = col_perm(lambda x, y, c: (x, y + 1 if c == 0 else y - 1, c))


def sent(value, perm, axis="col"):
    return lax.ppermute(value, axis, perm)


def payload(slots, block_list, col_blocks):
    me = lax.axis_index("col")
    clipped = jnp.maximum(block_list, 0)
    band_block = me * col_blocks + clipped % col_blocks
    pair_block = jnp.where(block_list >= 0, clipped // col_blocks, PAIR_BLOCKS)
    row = jnp.concatenate(
        [
            jnp.pad(band_block, (0, P_LANE - KMAX)),
            jnp.pad(pair_block, (0, BLK - P_LANE - KMAX)),
        ]
    )
    rows = jnp.broadcast_to(row.astype(jnp.bfloat16), (LIST_ROWS, BLK))
    return jnp.concatenate([slots.reshape(SLOT_ROWS, BLK), rows])[None]


def add_products(metric_ref, piece_refs, total, metric_v, pieces_v, rows_v, list_v, list_s, sems, prepare):
    starts = [sum(ref.shape[0] for ref in piece_refs[:n]) for n in range(len(piece_refs))]
    places = [pl.ds(start, ref.shape[0]) for start, ref in zip(starts, piece_refs)]
    list_rows = [
        pltpu.make_async_copy(ref.at[:, SLOT_ROWS:, :], rows_v.at[place], sems.at[0, n])
        for n, (ref, place) in enumerate(zip(piece_refs, places))
    ]
    metric_copy = pltpu.make_async_copy(metric_ref, metric_v, sems.at[1, len(piece_refs)])
    piece_copies = [
        pltpu.make_async_copy(ref.at[:, :SLOT_ROWS, :], pieces_v.at[place], sems.at[1, n])
        for n, (ref, place) in enumerate(zip(piece_refs, places))
    ]
    for copy in (*list_rows, metric_copy, *piece_copies):
        copy.start()
    for copy in list_rows:
        copy.wait()
    for i in range(rows_v.shape[0]):
        rows = rows_v[i].astype(jnp.float32)
        list_v[i : i + 1, :] = rows[:1].astype(jnp.int32)
    list_copy = pltpu.make_async_copy(list_v, list_s, sems.at[0, len(piece_refs)])
    list_copy.start()
    prepare()
    list_copy.wait()
    metric_copy.wait()

    def one_piece(i, carry):
        for j in range(KMAX):
            band_block = list_s[i, j]
            pair_block = list_s[i, P_LANE + j]
            prod = jnp.dot(
                pieces_v[i, j * BLK : (j + 1) * BLK, :],
                metric_v[band_block],
                preferred_element_type=jnp.float32,
            )
            total[pair_block] += prod
        return carry

    for copy, start, ref in zip(piece_copies, starts, piece_refs):
        copy.wait()
        lax.fori_loop(start, start + ref.shape[0], one_piece, 0, unroll=min(2, ref.shape[0]))


def early_products(metric_ref, *refs):
    *piece_refs, total, metric_v, pieces_v, rows_v, list_v, list_s, sems = refs

    def clear():
        total[...] = jnp.zeros_like(total)

    add_products(metric_ref, piece_refs, total, metric_v, pieces_v, rows_v, list_v, list_s, sems, clear)


def late_products(early_ref, metric_ref, *refs):
    *piece_refs, out_ref, total, total_sem, metric_v, pieces_v, rows_v, list_v, list_s, sems = refs
    taken = pltpu.make_async_copy(early_ref, total, total_sem)
    taken.start()
    add_products(
        metric_ref, piece_refs, total, metric_v, pieces_v, rows_v, list_v, list_s, sems, taken.wait
    )
    given = pltpu.make_async_copy(total.at[:PAIR_BLOCKS], out_ref, total_sem)
    given.start()
    given.wait()


def kernel_call(body, out_shape, out_space, taken, metric, pieces, scratch):
    count = sum(piece.shape[0] for piece in pieces)
    return pl.pallas_call(
        body,
        out_shape=out_shape,
        in_specs=[pl.BlockSpec(memory_space=pltpu.HBM)] * (len(taken) + 1 + len(pieces)),
        out_specs=pl.BlockSpec(memory_space=out_space),
        scratch_shapes=[
            *scratch,
            pltpu.VMEM(metric.shape, metric.dtype),
            pltpu.VMEM((count, SLOT_ROWS, BLK), metric.dtype),
            pltpu.VMEM((count, LIST_ROWS, BLK), metric.dtype),
            pltpu.VMEM((count, BLK), jnp.int32),
            pltpu.SMEM((count, BLK), jnp.int32),
            pltpu.SemaphoreType.DMA((2, len(pieces) + 1)),
        ],
        compiler_params=pltpu.CompilerParams(vmem_limit_bytes=60 << 20),
    )(*taken, metric, *pieces)


def copy_to_each(source_ref, copies_ref, source_v, sems):
    count = copies_ref.shape[0]
    taken = pltpu.make_async_copy(source_ref, source_v, sems.at[count])
    taken.start()
    taken.wait()
    copies = [pltpu.make_async_copy(source_v, copies_ref.at[i], sems.at[i]) for i in range(count)]
    for copy in copies:
        copy.start()
    for copy in copies:
        copy.wait()


def on_device(slots, block_list, metric):
    out_cols = metric.shape[1]
    rows = lax.axis_size("row")
    band_blocks = rows * metric.shape[0] // BLK
    col_blocks = band_blocks // lax.axis_size("col")
    copies = pl.pallas_call(
        copy_to_each,
        out_shape=jax.ShapeDtypeStruct((rows, *metric.shape), metric.dtype),
        in_specs=[pl.BlockSpec(memory_space=pltpu.HBM)],
        out_specs=pl.BlockSpec(memory_space=pltpu.HBM),
        scratch_shapes=[pltpu.VMEM(metric.shape, metric.dtype), pltpu.SemaphoreType.DMA((rows + 1,))],
    )(metric)
    band = lax.all_to_all(copies, "row", split_axis=0, concat_axis=0, tiled=True)
    band = band.reshape(band_blocks, BLK, out_cols)

    own = payload(slots, block_list, col_blocks)
    own_x = sent(own, X_PARTNER)
    near = jnp.concatenate([own, sent(own, CORE)])
    near_x = jnp.concatenate([own_x, sent(own_x, CORE)])
    a1 = sent(near, RING)
    b1 = sent(near_x, RING)
    a2 = sent(a1, RING)
    b2 = sent(b1, RING)
    a3 = sent(a2, RING)
    a4 = sent(a3[:1], RING)
    early = [a1, b1, a2, b2, a3]
    late = [sent(a3, X_PARTNER), a4, sent(a4, X_PARTNER)]
    early_other = sent(jnp.concatenate(early), CORE)
    late_other = sent(jnp.concatenate(late), CORE)
    early = [near, near_x, *early, early_other]
    late = [*late, late_other]
    total_shape = (PAIR_BLOCKS + 1, BLK, out_cols)
    total = kernel_call(
        early_products,
        jax.ShapeDtypeStruct(total_shape, jnp.float32),
        pltpu.VMEM,
        [],
        band,
        early,
        [],
    )
    blocks = kernel_call(
        late_products,
        jax.ShapeDtypeStruct((PAIR_BLOCKS, BLK, out_cols), jnp.float32),
        pltpu.HBM,
        [total],
        band,
        late,
        [pltpu.VMEM(total_shape, jnp.float32), pltpu.SemaphoreType.DMA],
    )
    return blocks.reshape(PAIR_DEV, out_cols)


def solution(mesh):
    return jax.shard_map(
        on_device,
        mesh=mesh,
        in_specs=(P(("row", "col"), None, None), P(("row", "col")), P("row", "col")),
        out_specs=P("row", "col"),
        check_vma=False,
    )
```

```python
import jax
import jax.numpy as jnp
from jax import lax
from jax.experimental import pallas as pl
from jax.experimental.pallas import tpu as pltpu
from jax.sharding import PartitionSpec as P

BLK = 128
PAIR_DEV = 1024
PAIR_BLOCKS = PAIR_DEV // BLK
KMAX = 6
NY = 8
LIST_ROWS = 16
SLOT_ROWS = KMAX * BLK
P_LANE = 8


def col_of(x, y, core):
    return ((x % 2) * NY + y % NY) * 2 + core % 2


def col_perm(target):
    return [
        (col_of(x, y, c), col_of(*target(x, y, c)))
        for x in range(2)
        for y in range(NY)
        for c in range(2)
    ]


CORE = col_perm(lambda x, y, c: (x, y, c + 1))
X_PARTNER = col_perm(lambda x, y, c: (x + 1, y, c))
RING = col_perm(lambda x, y, c: (x, y + 1 if c == 0 else y - 1, c))


def sent(value, perm, axis="col"):
    return lax.ppermute(value, axis, perm)


def payload(slots, block_list, col_blocks):
    me = lax.axis_index("col")
    clipped = jnp.maximum(block_list, 0)
    band_block = me * col_blocks + clipped % col_blocks
    pair_block = jnp.where(block_list >= 0, clipped // col_blocks, PAIR_BLOCKS)
    row = jnp.concatenate(
        [
            jnp.pad(band_block, (0, P_LANE - KMAX)),
            jnp.pad(pair_block, (0, BLK - P_LANE - KMAX)),
        ]
    )
    rows = jnp.broadcast_to(row.astype(jnp.bfloat16), (LIST_ROWS, BLK))
    return jnp.concatenate([slots.reshape(SLOT_ROWS, BLK), rows])[None]


def add_products(metric_ref, piece_refs, total, metric_v, pieces_v, rows_v, list_v, list_s, sems, prepare):
    starts = [sum(ref.shape[0] for ref in piece_refs[:n]) for n in range(len(piece_refs))]
    places = [pl.ds(start, ref.shape[0]) for start, ref in zip(starts, piece_refs)]
    list_rows = [
        pltpu.make_async_copy(ref.at[:, SLOT_ROWS:, :], rows_v.at[place], sems.at[0, n])
        for n, (ref, place) in enumerate(zip(piece_refs, places))
    ]
    metric_copies = []
    if metric_v is not None:
        metric_copies = [pltpu.make_async_copy(metric_ref, metric_v, sems.at[1, len(piece_refs)])]
    band = metric_ref if metric_v is None else metric_v
    piece_copies = [
        pltpu.make_async_copy(ref.at[:, :SLOT_ROWS, :], pieces_v.at[place], sems.at[1, n])
        for n, (ref, place) in enumerate(zip(piece_refs, places))
    ]
    for copy in (*list_rows, *metric_copies, *piece_copies):
        copy.start()
    for copy in list_rows:
        copy.wait()
    for i in range(rows_v.shape[0]):
        rows = rows_v[i].astype(jnp.float32)
        list_v[i : i + 1, :] = rows[:1].astype(jnp.int32)
    list_copy = pltpu.make_async_copy(list_v, list_s, sems.at[0, len(piece_refs)])
    list_copy.start()
    prepare()
    list_copy.wait()
    for copy in metric_copies:
        copy.wait()

    def one_piece(i, carry):
        for j in range(KMAX):
            band_block = list_s[i, j]
            pair_block = list_s[i, P_LANE + j]
            prod = jnp.dot(
                pieces_v[i, j * BLK : (j + 1) * BLK, :],
                band[band_block],
                preferred_element_type=jnp.float32,
            )
            total[pair_block] += prod
        return carry

    for copy in piece_copies:
        copy.wait()
    lax.fori_loop(0, rows_v.shape[0], one_piece, 0, unroll=2)


def early_products(metric_ref, *refs):
    *piece_refs, total, pieces_v, rows_v, list_v, list_s, sems = refs

    def clear():
        total[...] = jnp.zeros_like(total)

    add_products(metric_ref, piece_refs, total, None, pieces_v, rows_v, list_v, list_s, sems, clear)


def late_products(early_ref, metric_ref, *refs):
    *piece_refs, out_ref, total, total_sem, metric_v, pieces_v, rows_v, list_v, list_s, sems = refs
    taken = pltpu.make_async_copy(early_ref, total, total_sem)
    taken.start()
    add_products(
        metric_ref, piece_refs, total, metric_v, pieces_v, rows_v, list_v, list_s, sems, taken.wait
    )
    given = pltpu.make_async_copy(total.at[:PAIR_BLOCKS], out_ref, total_sem)
    given.start()
    given.wait()


def kernel_call(body, limit, out_shape, out_space, band_space, taken, metric, pieces, scratch):
    count = sum(piece.shape[0] for piece in pieces)
    return pl.pallas_call(
        body,
        out_shape=out_shape,
        in_specs=[pl.BlockSpec(memory_space=pltpu.HBM)] * len(taken)
        + [pl.BlockSpec(memory_space=band_space)]
        + [pl.BlockSpec(memory_space=pltpu.HBM)] * len(pieces),
        out_specs=pl.BlockSpec(memory_space=out_space),
        scratch_shapes=[
            *scratch,
            pltpu.VMEM((count, SLOT_ROWS, BLK), metric.dtype),
            pltpu.VMEM((count, LIST_ROWS, BLK), metric.dtype),
            pltpu.VMEM((count, BLK), jnp.int32),
            pltpu.SMEM((count, BLK), jnp.int32),
            pltpu.SemaphoreType.DMA((2, len(pieces) + 1)),
        ],
        compiler_params=pltpu.CompilerParams(vmem_limit_bytes=limit << 20),
    )(*taken, metric, *pieces)


def copy_to_each(source_ref, copies_ref, sems):
    count = copies_ref.shape[0]
    copies = [pltpu.make_async_copy(source_ref, copies_ref.at[i], sems.at[i]) for i in range(count)]
    for copy in copies:
        copy.start()
    for copy in copies:
        copy.wait()


def on_device(slots, block_list, metric):
    out_cols = metric.shape[1]
    rows = lax.axis_size("row")
    band_blocks = rows * metric.shape[0] // BLK
    col_blocks = band_blocks // lax.axis_size("col")
    copies = pl.pallas_call(
        copy_to_each,
        out_shape=jax.ShapeDtypeStruct((rows, *metric.shape), metric.dtype),
        in_specs=[pl.BlockSpec(memory_space=pltpu.HBM)],
        out_specs=pl.BlockSpec(memory_space=pltpu.HBM),
        scratch_shapes=[pltpu.SemaphoreType.DMA((rows,))],
    )(metric)
    band = lax.all_to_all(copies, "row", split_axis=0, concat_axis=0, tiled=True)
    band = band.reshape(band_blocks, BLK, out_cols)

    own = payload(slots, block_list, col_blocks)
    own_x = sent(own, X_PARTNER)
    near = jnp.concatenate([own, sent(own, CORE)])
    near_x = jnp.concatenate([own_x, sent(own_x, CORE)])
    a1 = sent(near, RING)
    b1 = sent(near_x, RING)
    a2 = sent(a1, RING)
    b2 = sent(b1, RING)
    a3 = sent(a2, RING)
    a4 = sent(a3[:1], RING)
    early = [a1, b1, a2, b2, a3]
    late = [sent(a3, X_PARTNER), a4, sent(a4, X_PARTNER)]
    early_other = sent(jnp.concatenate(early), CORE)
    late_other = sent(jnp.concatenate(late), CORE)
    early = [near, near_x, *early, early_other]
    late = [*late, late_other]
    total_shape = (PAIR_BLOCKS + 1, BLK, out_cols)
    total = kernel_call(
        early_products,
        52,
        jax.ShapeDtypeStruct(total_shape, jnp.float32),
        pltpu.VMEM,
        pltpu.VMEM,
        [],
        pltpu.with_memory_space_constraint(band, pltpu.VMEM),
        early,
        [],
    )
    blocks = kernel_call(
        late_products,
        40,
        jax.ShapeDtypeStruct((PAIR_BLOCKS, BLK, out_cols), jnp.float32),
        pltpu.HBM,
        pltpu.HBM,
        [total],
        band,
        late,
        [
            pltpu.VMEM(total_shape, jnp.float32),
            pltpu.SemaphoreType.DMA,
            pltpu.VMEM(band.shape, band.dtype),
        ],
    )
    return blocks.reshape(PAIR_DEV, out_cols)


def solution(mesh):
    return jax.shard_map(
        on_device,
        mesh=mesh,
        in_specs=(P(("row", "col"), None, None), P(("row", "col")), P("row", "col")),
        out_specs=P("row", "col"),
        check_vma=False,
    )
```

```python
import jax
import jax.numpy as jnp
from jax import lax
from jax.experimental import pallas as pl
from jax.experimental.pallas import tpu as pltpu
from jax.sharding import PartitionSpec as P

BLK = 128
PAIR_DEV = 1024
PAIR_BLOCKS = PAIR_DEV // BLK
KMAX = 6
NY = 8
LIST_ROWS = 16
SLOT_ROWS = KMAX * BLK
UNIT = SLOT_ROWS + LIST_ROWS
P_LANE = 8


def col_of(x, y, core):
    return ((x % 2) * NY + y % NY) * 2 + core % 2


def col_perm(target):
    return [
        (col_of(x, y, c), col_of(*target(x, y, c)))
        for x in range(2)
        for y in range(NY)
        for c in range(2)
    ]


CORE = col_perm(lambda x, y, c: (x, y, c + 1))
X_PARTNER = col_perm(lambda x, y, c: (x + 1, y, c))
RING = col_perm(lambda x, y, c: (x, y + 1 if c == 0 else y - 1, c))


def sent(value, perm, axis="col"):
    return lax.ppermute(value, axis, perm)


def add_products(metric_ref, piece_refs, total, metric_v, pieces_v, rows_v, list_v, list_s, sems, prepare):
    starts = [sum(ref.shape[0] for ref in piece_refs[:n]) for n in range(len(piece_refs))]
    places = [pl.ds(start, ref.shape[0]) for start, ref in zip(starts, piece_refs)]
    list_rows = [
        pltpu.make_async_copy(ref.at[:, SLOT_ROWS:, :], rows_v.at[place], sems.at[0, n])
        for n, (ref, place) in enumerate(zip(piece_refs, places))
    ]
    metric_copies = []
    if metric_v is not None:
        metric_copies = [pltpu.make_async_copy(metric_ref, metric_v, sems.at[1, len(piece_refs)])]
    band = metric_ref if metric_v is None else metric_v
    piece_copies = [
        pltpu.make_async_copy(ref.at[:, :SLOT_ROWS, :], pieces_v.at[place], sems.at[1, n])
        for n, (ref, place) in enumerate(zip(piece_refs, places))
    ]
    for copy in (*list_rows, *metric_copies, *piece_copies):
        copy.start()
    for copy in list_rows:
        copy.wait()
    for i in range(rows_v.shape[0]):
        rows = rows_v[i].astype(jnp.float32)
        list_v[i : i + 1, :] = rows[:1].astype(jnp.int32)
    list_copy = pltpu.make_async_copy(list_v, list_s, sems.at[0, len(piece_refs)])
    list_copy.start()
    prepare()
    list_copy.wait()
    for copy in metric_copies:
        copy.wait()

    def one_piece(i, carry):
        for j in range(KMAX):
            band_block = list_s[i, j]
            pair_block = list_s[i, P_LANE + j]
            prod = jnp.dot(
                pieces_v[i, j * BLK : (j + 1) * BLK, :],
                band[band_block],
                preferred_element_type=jnp.float32,
            )
            total[pair_block] += prod
        return carry

    start, end = 0, 0
    for copy, ref in zip(piece_copies, piece_refs):
        copy.wait()
        end += ref.shape[0]
        if (end - start) % 2 == 0:
            lax.fori_loop(start, end, one_piece, 0, unroll=2)
            start = end


def early_products(metric_ref, *refs):
    *piece_refs, total, pieces_v, rows_v, list_v, list_s, sems = refs

    def clear():
        total[...] = jnp.zeros_like(total)

    add_products(metric_ref, piece_refs, total, None, pieces_v, rows_v, list_v, list_s, sems, clear)


def late_products(early_ref, metric_ref, *refs):
    *piece_refs, out_ref, total, total_sem, metric_v, pieces_v, rows_v, list_v, list_s, sems = refs
    taken = pltpu.make_async_copy(early_ref, total, total_sem)
    taken.start()
    add_products(
        metric_ref, piece_refs, total, metric_v, pieces_v, rows_v, list_v, list_s, sems, taken.wait
    )
    given = pltpu.make_async_copy(total.at[:PAIR_BLOCKS], out_ref, total_sem)
    given.start()
    given.wait()


def kernel_call(body, limit, out_shape, out_space, band_space, taken, metric, pieces, scratch):
    count = sum(piece.shape[0] for piece in pieces)
    return pl.pallas_call(
        body,
        out_shape=out_shape,
        in_specs=[pl.BlockSpec(memory_space=pltpu.HBM)] * len(taken)
        + [pl.BlockSpec(memory_space=band_space)]
        + [pl.BlockSpec(memory_space=pltpu.HBM)] * len(pieces),
        out_specs=pl.BlockSpec(memory_space=out_space),
        scratch_shapes=[
            *scratch,
            pltpu.VMEM((count, SLOT_ROWS, BLK), metric.dtype),
            pltpu.VMEM((count, LIST_ROWS, BLK), metric.dtype),
            pltpu.VMEM((count, BLK), jnp.int32),
            pltpu.SMEM((count, BLK), jnp.int32),
            pltpu.SemaphoreType.DMA((2, len(pieces) + 1)),
        ],
        compiler_params=pltpu.CompilerParams(vmem_limit_bytes=limit << 20),
    )(*taken, metric, *pieces)


def prepare_sends(list_ref, metric_ref, slots_ref, copies_ref, payload_ref, metric_v, payload_v, sems):
    count = copies_ref.shape[0]
    metric_in = pltpu.make_async_copy(metric_ref, metric_v, sems.at[count])
    metric_in.start()
    slots_in = [
        pltpu.make_async_copy(
            slots_ref.at[j], payload_v.at[0, j * BLK : (j + 1) * BLK, :], sems.at[count + 1 + j]
        )
        for j in range(KMAX)
    ]
    for copy in slots_in:
        copy.start()
    band_blocks = count * metric_ref.shape[0] // BLK
    col_blocks = band_blocks // lax.axis_size("col")
    first_block = lax.axis_index("col") * col_blocks
    lanes = lax.broadcasted_iota(jnp.int32, (LIST_ROWS, BLK), 1)
    rows = jnp.zeros((LIST_ROWS, BLK), jnp.int32)
    for j in range(KMAX):
        entry = list_ref[j]
        used = jnp.maximum(entry, 0)
        pair_block = jnp.where(entry >= 0, used // col_blocks, PAIR_BLOCKS)
        rows = jnp.where(lanes == j, first_block + used % col_blocks, rows)
        rows = jnp.where(lanes == P_LANE + j, pair_block, rows)
    payload_v[0, SLOT_ROWS:, :] = rows.astype(jnp.float32).astype(payload_v.dtype)
    metric_in.wait()
    copies = [pltpu.make_async_copy(metric_v, copies_ref.at[i], sems.at[i]) for i in range(count)]
    for copy in copies:
        copy.start()
    for copy in slots_in:
        copy.wait()
    payload_out = pltpu.make_async_copy(payload_v, payload_ref, sems.at[count])
    payload_out.start()
    for copy in copies:
        copy.wait()
    payload_out.wait()


def on_device(slots, block_list, metric):
    out_cols = metric.shape[1]
    rows = lax.axis_size("row")
    band_blocks = rows * metric.shape[0] // BLK
    hbm = pl.BlockSpec(memory_space=pltpu.HBM)
    payload_shape = (1, UNIT, BLK)
    copies, own = pl.pallas_call(
        prepare_sends,
        out_shape=(
            jax.ShapeDtypeStruct((rows, *metric.shape), metric.dtype),
            jax.ShapeDtypeStruct(payload_shape, slots.dtype),
        ),
        in_specs=[pl.BlockSpec(memory_space=pltpu.SMEM), hbm, hbm],
        out_specs=(hbm, hbm),
        scratch_shapes=[
            pltpu.VMEM(metric.shape, metric.dtype),
            pltpu.VMEM(payload_shape, slots.dtype),
            pltpu.SemaphoreType.DMA((rows + 1 + KMAX,)),
        ],
        compiler_params=pltpu.CompilerParams(vmem_limit_bytes=60 << 20),
    )(block_list, metric, slots)
    band = lax.all_to_all(copies, "row", split_axis=0, concat_axis=0, tiled=True)
    band = band.reshape(band_blocks, BLK, out_cols)

    own_x = sent(own, X_PARTNER)
    near = jnp.concatenate([own, sent(own, CORE)])
    near_x = jnp.concatenate([own_x, sent(own_x, CORE)])
    a1 = sent(near, RING)
    b1 = sent(near_x, RING)
    a2 = sent(a1, RING)
    b2 = sent(b1, RING)
    a3 = sent(a2, RING)
    a4 = sent(a3[:1], RING)
    b3 = sent(b2, RING)
    b4 = sent(b3[:1], RING)
    early_other = sent(jnp.concatenate([a1, b1, a2, b2, a3]), CORE)
    late_other = sent(jnp.concatenate([b3, a4, b4]), CORE)
    early = [near, near_x, a1, b1, a2, b2, a3, early_other]
    late = [b3, a4, b4, late_other]
    total_shape = (PAIR_BLOCKS + 1, BLK, out_cols)
    total = kernel_call(
        early_products,
        52,
        jax.ShapeDtypeStruct(total_shape, jnp.float32),
        pltpu.VMEM,
        pltpu.VMEM,
        [],
        pltpu.with_memory_space_constraint(band, pltpu.VMEM),
        early,
        [],
    )
    blocks = kernel_call(
        late_products,
        40,
        jax.ShapeDtypeStruct((PAIR_BLOCKS, BLK, out_cols), jnp.float32),
        pltpu.HBM,
        pltpu.HBM,
        [total],
        band,
        late,
        [
            pltpu.VMEM(total_shape, jnp.float32),
            pltpu.SemaphoreType.DMA,
            pltpu.VMEM(band.shape, band.dtype),
        ],
    )
    return blocks.reshape(PAIR_DEV, out_cols)


def solution(mesh):
    return jax.shard_map(
        on_device,
        mesh=mesh,
        in_specs=(P(("row", "col"), None, None), P(("row", "col")), P("row", "col")),
        out_specs=P("row", "col"),
        check_vma=False,
    )
```

```python
import jax
import jax.numpy as jnp
from jax import lax
from jax.experimental import pallas as pl
from jax.experimental.pallas import tpu as pltpu
from jax.sharding import PartitionSpec as P

BLK = 128
PAIR_DEV = 1024
PAIR_BLOCKS = PAIR_DEV // BLK
KMAX = 6
NY = 8
LIST_ROWS = 16
SLOT_ROWS = KMAX * BLK
P_LANE = 8


def col_of(x, y, core):
    return ((x % 2) * NY + y % NY) * 2 + core % 2


def col_perm(target):
    return [
        (col_of(x, y, c), col_of(*target(x, y, c)))
        for x in range(2)
        for y in range(NY)
        for c in range(2)
    ]


CORE = col_perm(lambda x, y, c: (x, y, c + 1))
X_PARTNER = col_perm(lambda x, y, c: (x + 1, y, c))
RING = col_perm(lambda x, y, c: (x, y + 1 if c == 0 else y - 1, c))


def sent(value, perm, axis="col"):
    return lax.ppermute(value, axis, perm)


def payload(slots, block_list, col_blocks):
    me = lax.axis_index("col")
    clipped = jnp.maximum(block_list, 0)
    band_block = me * col_blocks + clipped % col_blocks
    pair_block = jnp.where(block_list >= 0, clipped // col_blocks, PAIR_BLOCKS)
    row = jnp.concatenate(
        [
            jnp.pad(band_block, (0, P_LANE - KMAX)),
            jnp.pad(pair_block, (0, BLK - P_LANE - KMAX)),
        ]
    )
    rows = jnp.broadcast_to(row.astype(jnp.bfloat16), (LIST_ROWS, BLK))
    return jnp.concatenate([slots.reshape(SLOT_ROWS, BLK), rows])[None]


def add_products(metric_ref, piece_refs, total, metric_v, pieces_v, rows_v, list_v, list_s, sems, prepare):
    starts = [sum(ref.shape[0] for ref in piece_refs[:n]) for n in range(len(piece_refs))]
    places = [pl.ds(start, ref.shape[0]) for start, ref in zip(starts, piece_refs)]
    list_rows = [
        pltpu.make_async_copy(ref.at[:, SLOT_ROWS:, :], rows_v.at[place], sems.at[0, n])
        for n, (ref, place) in enumerate(zip(piece_refs, places))
    ]
    metric_copies = []
    if metric_v is not None:
        metric_copies = [pltpu.make_async_copy(metric_ref, metric_v, sems.at[1, len(piece_refs)])]
    band = metric_ref if metric_v is None else metric_v
    piece_copies = [
        pltpu.make_async_copy(ref.at[:, :SLOT_ROWS, :], pieces_v.at[place], sems.at[1, n])
        for n, (ref, place) in enumerate(zip(piece_refs, places))
    ]
    for copy in (*list_rows, *metric_copies, *piece_copies):
        copy.start()
    for copy in list_rows:
        copy.wait()
    for i in range(rows_v.shape[0]):
        rows = rows_v[i].astype(jnp.float32)
        list_v[i : i + 1, :] = rows[:1].astype(jnp.int32)
    list_copy = pltpu.make_async_copy(list_v, list_s, sems.at[0, len(piece_refs)])
    list_copy.start()
    prepare()
    list_copy.wait()
    for copy in metric_copies:
        copy.wait()

    def one_piece(i, carry):
        for j in range(KMAX):
            band_block = list_s[i, j]
            pair_block = list_s[i, P_LANE + j]
            prod = jnp.dot(
                pieces_v[i, j * BLK : (j + 1) * BLK, :],
                band[band_block],
                preferred_element_type=jnp.float32,
            )
            total[pair_block] += prod
        return carry

    start, end = 0, 0
    for copy, ref in zip(piece_copies, piece_refs):
        copy.wait()
        end += ref.shape[0]
        if (end - start) % 2 == 0:
            length = end - start
            step = max(n for n in (2, 3, 4) if length % n == 0)
            lax.fori_loop(start, end, one_piece, 0, unroll=step)
            start = end


def early_products(metric_ref, *refs):
    *piece_refs, total, pieces_v, rows_v, list_v, list_s, sems = refs

    def clear():
        total[...] = jnp.zeros_like(total)

    add_products(metric_ref, piece_refs, total, None, pieces_v, rows_v, list_v, list_s, sems, clear)


def late_products(early_ref, metric_ref, *refs):
    *piece_refs, out_ref, total, total_sem, metric_v, pieces_v, rows_v, list_v, list_s, sems = refs
    taken = pltpu.make_async_copy(early_ref, total, total_sem)
    taken.start()
    add_products(
        metric_ref, piece_refs, total, metric_v, pieces_v, rows_v, list_v, list_s, sems, taken.wait
    )
    given = pltpu.make_async_copy(total.at[:PAIR_BLOCKS], out_ref, total_sem)
    given.start()
    given.wait()


def kernel_call(body, limit, out_shape, out_space, band_space, taken, metric, pieces, scratch):
    count = sum(piece.shape[0] for piece in pieces)
    return pl.pallas_call(
        body,
        out_shape=out_shape,
        in_specs=[pl.BlockSpec(memory_space=pltpu.HBM)] * len(taken)
        + [pl.BlockSpec(memory_space=band_space)]
        + [pl.BlockSpec(memory_space=pltpu.HBM)] * len(pieces),
        out_specs=pl.BlockSpec(memory_space=out_space),
        scratch_shapes=[
            *scratch,
            pltpu.VMEM((count, SLOT_ROWS, BLK), metric.dtype),
            pltpu.VMEM((count, LIST_ROWS, BLK), metric.dtype),
            pltpu.VMEM((count, BLK), jnp.int32),
            pltpu.SMEM((count, BLK), jnp.int32),
            pltpu.SemaphoreType.DMA((2, len(pieces) + 1)),
        ],
        compiler_params=pltpu.CompilerParams(vmem_limit_bytes=limit << 20),
    )(*taken, metric, *pieces)


def copy_to_each(source_ref, copies_ref, source_v, sems):
    count = copies_ref.shape[0]
    taken = pltpu.make_async_copy(source_ref, source_v, sems.at[count])
    taken.start()
    taken.wait()
    copies = [pltpu.make_async_copy(source_v, copies_ref.at[i], sems.at[i]) for i in range(count)]
    for copy in copies:
        copy.start()
    for copy in copies:
        copy.wait()


def on_device(slots, block_list, metric):
    out_cols = metric.shape[1]
    rows = lax.axis_size("row")
    band_blocks = rows * metric.shape[0] // BLK
    col_blocks = band_blocks // lax.axis_size("col")
    copies = pl.pallas_call(
        copy_to_each,
        out_shape=jax.ShapeDtypeStruct((rows, *metric.shape), metric.dtype),
        in_specs=[pl.BlockSpec(memory_space=pltpu.HBM)],
        out_specs=pl.BlockSpec(memory_space=pltpu.HBM),
        scratch_shapes=[pltpu.VMEM(metric.shape, metric.dtype), pltpu.SemaphoreType.DMA((rows + 1,))],
    )(metric)
    band = lax.all_to_all(copies, "row", split_axis=0, concat_axis=0, tiled=True)
    band = band.reshape(band_blocks, BLK, out_cols)

    own = payload(slots, block_list, col_blocks)
    own_x = sent(own, X_PARTNER)
    near = jnp.concatenate([own, sent(own, CORE)])
    near_x = jnp.concatenate([own_x, sent(own_x, CORE)])
    a1 = sent(near, RING)
    b1 = sent(near_x, RING)
    a2 = sent(a1, RING)
    b2 = sent(b1, RING)
    a3 = sent(a2, RING)
    a4 = sent(a3[:1], RING)
    b3 = sent(b2, RING)
    a4_x = sent(a4, X_PARTNER)
    early_other = sent(jnp.concatenate([a1, b1, a2, a3]), CORE)
    late_other = sent(jnp.concatenate([b2, b3, a4, a4_x]), CORE)
    early = [near, near_x, a1, b1, a2, a3, early_other]
    late = [b2, b3, a4, a4_x, late_other]
    total_shape = (PAIR_BLOCKS + 1, BLK, out_cols)
    total = kernel_call(
        early_products,
        52,
        jax.ShapeDtypeStruct(total_shape, jnp.float32),
        pltpu.VMEM,
        pltpu.VMEM,
        [],
        pltpu.with_memory_space_constraint(band, pltpu.VMEM),
        early,
        [],
    )
    blocks = kernel_call(
        late_products,
        40,
        jax.ShapeDtypeStruct((PAIR_BLOCKS, BLK, out_cols), jnp.float32),
        pltpu.HBM,
        pltpu.HBM,
        [total],
        band,
        late,
        [
            pltpu.VMEM(total_shape, jnp.float32),
            pltpu.SemaphoreType.DMA,
            pltpu.VMEM(band.shape, band.dtype),
        ],
    )
    return blocks.reshape(PAIR_DEV, out_cols)


def solution(mesh):
    return jax.shard_map(
        on_device,
        mesh=mesh,
        in_specs=(P(("row", "col"), None, None), P(("row", "col")), P("row", "col")),
        out_specs=P("row", "col"),
        check_vma=False,
    )
```
